32 devices in a mesh: groups: 2 (over y), shard: 4 (over z), pair: 4 (over x, core).
Axes of the slice: x: 2, y: 2, z: 4, core: 2. Of those that a mesh axis runs over, the one named last changes fastest.
Arguments:
- gradient: bfloat16 [2, 8, 512, 512], P('groups', None, 'shard'), parts along dimension 0, may hold values from -6.5 to 6.5, as said below
- momentum: bfloat16 [2, 8, 512, 512], P('groups', None, 'shard'), parts along dimension 0, may hold values from -6.5 to 6.5, as said below
Outputs:
- update: bfloat16 [2, 8, 512, 512], P('groups', None, 'shard'), parts along dimension 0
- new_momentum: bfloat16 [2, 8, 512, 512], P('groups', None, 'shard'), parts along dimension 0
The draws below stay inside these ranges and needn't reach their ends.
There are 2 independent parts, one for each index of `groups`. The reference program is written for one: setup_inputs(seed, part) draws one part's arguments, and reference() takes and returns one part's arrays. A program takes and returns all parts, laid end to end along the dimension named above; each array names one. Nothing has to cross between parts.
Inputs may be any that keep to these rules, and one draw needn't show every extreme that they name: `gradient`: entries of order one. `momentum`: entries of order one.
All inputs are finite; a program needn't handle non-finite values.
Results may differ from the reference program's by a relative error of at most 0.0053.
Values may be sent and summed in bfloat16 or wider, within the bound.
A program may use at most 64 MiB of HBM per device.

```python
import jax
import jax.numpy as jnp
from jax import lax

BLK = 512
BCOL = 8
BROW = 1


def block_entries(key, salt):
    inner = jax.random.fold_in(key, salt)
    base_key = jax.random.fold_in(inner, 0)
    full_shape = (BROW, BCOL, BLK, BLK)
    values = jax.random.truncated_normal(base_key, -6.0, 6.0, full_shape, jnp.float32)
    return values.astype(jnp.bfloat16)


def draw_gradient(key, part):
    return block_entries(key, 101)


def draw_momentum(key, part):
    return block_entries(key, 202)


def setup_inputs(seed: int = 0, part: int = 0) -> dict:
    splits = jax.random.split(jax.random.key(seed), 3)
    own_keys = jax.random.split(jax.random.fold_in(splits[2], part), 3)
    gradient = draw_gradient(jax.random.fold_in(jax.random.fold_in(splits[2], part), 71), part)
    momentum = draw_momentum(jax.random.fold_in(jax.random.fold_in(splits[2], part), 71), part)
    return {"gradient": gradient, "momentum": momentum}


damping = 0.1
decay_rate = 0.9

def multiply(left_matrix, right_matrix):
    return jnp.dot(left_matrix, right_matrix, precision=lax.Precision.HIGHEST, preferred_element_type=jnp.float32)

def gram_root(gram_matrix):
    block_size = gram_matrix.shape[0]
    identity = jnp.eye(block_size, dtype=jnp.float32)
    scaling = 2.0 * jnp.trace(gram_matrix) / block_size
    root_scale = jnp.sqrt(jnp.sqrt(scaling))
    scaled = gram_matrix / scaling
    leading = (5.0 * identity - scaled) / 4.0
    iterate = leading / root_scale
    squared = multiply(leading, leading)
    fourth = multiply(squared, squared)
    shifted = multiply(fourth, scaled)
    second = (5.0 * identity - shifted) / 4.0
    return multiply(iterate, second)

def reference(gradient, momentum):
    new_momentum = (decay_rate * momentum.astype(jnp.float32) + gradient.astype(jnp.float32)).astype(jnp.bfloat16)
    grad_blocks = gradient.reshape(-1, BLK, BLK)
    mom_blocks = new_momentum.reshape(-1, BLK, BLK)
    identity = jnp.eye(BLK, dtype=jnp.float32)

    def one_block(blocks_pair):
        grad_block, mom_block = blocks_pair
        left_gram = jnp.dot(grad_block, grad_block.T, preferred_element_type=jnp.float32) / BLK + damping * identity
        right_gram = jnp.dot(grad_block.T, grad_block, preferred_element_type=jnp.float32) / BLK + damping * identity
        left_root = gram_root(left_gram)
        right_root = gram_root(right_gram)
        partial_prod = multiply(mom_block.astype(jnp.float32), right_root)
        return multiply(left_root, partial_prod).astype(jnp.bfloat16)
    updates = lax.map(one_block, (grad_blocks, mom_blocks)).reshape(gradient.shape)
    return (updates, new_momentum)
```

```python
import functools

import jax
import jax.numpy as jnp
from jax import lax
from jax.experimental import pallas as pl
from jax.experimental.pallas import tpu as pltpu
from jax.sharding import PartitionSpec as P

damping = 0.1
decay_rate = 0.9
MESH = pl.DeviceIdType.MESH


def from_partner(value, axis, apart):
    mask = 2**apart
    pairs = [(source, source ^ mask) for source in range(lax.axis_size(axis))]
    return lax.ppermute(value, axis, pairs)


def multiply(left_matrix, right_matrix):
    return jnp.dot(
        left_matrix,
        right_matrix,
        precision=lax.Precision.HIGHEST,
        preferred_element_type=jnp.float32,
    )


def gram_root(gram_matrix):
    block_size = gram_matrix.shape[0]
    identity = jnp.eye(block_size, dtype=jnp.float32)
    scaling = 2.0 * jnp.trace(gram_matrix) / block_size
    root_scale = jnp.sqrt(jnp.sqrt(scaling))
    scaled = gram_matrix / scaling
    leading = (5.0 * identity - scaled) / 4.0
    iterate = leading / root_scale
    squared = multiply(leading, leading)
    fourth = multiply(squared, squared)
    shifted = multiply(fourth, scaled)
    second = (5.0 * identity - shifted) / 4.0
    return multiply(iterate, second)


def by_collectives(gradient, momentum):
    new_momentum = (
        decay_rate * momentum.astype(jnp.float32) + gradient.astype(jnp.float32)
    ).astype(jnp.bfloat16)
    block_rows, block_cols, local_rows, block_size = gradient.shape
    half_cols = block_cols // 2
    half_width = block_size // 2
    shards = lax.axis_size("shard")
    position = lax.axis_index("pair")
    column_half = position // 2
    side_index = position % 2
    leading_side = side_index == 0
    grad_half = lax.dynamic_slice_in_dim(gradient, column_half * half_cols, half_cols, 1).reshape(
        shards, local_rows, block_size
    )
    mom_half = lax.dynamic_slice_in_dim(
        new_momentum, column_half * half_cols, half_cols, 1
    ).reshape(shards, local_rows, block_size)
    grad_recv, mom_recv = (
        lax.all_to_all(grad_half, "shard", split_axis=0, concat_axis=1, tiled=True),
        lax.all_to_all(mom_half, "shard", split_axis=0, concat_axis=1, tiled=True),
    )
    grad_block = grad_recv[0]
    mom_block = mom_recv[0]
    identity = jnp.eye(block_size, dtype=jnp.float32)
    oriented = jnp.where(leading_side, grad_block, grad_block.T)
    gram_matrix = (
        jnp.dot(oriented, oriented.T, preferred_element_type=jnp.float32) / block_size
        + damping * identity
    )
    own_root = gram_root(gram_matrix)
    partner = from_partner(own_root, "pair", 0)
    left_root = jnp.where(leading_side, own_root, partner)
    right_root = jnp.where(leading_side, partner, own_root)
    right_part = lax.dynamic_slice_in_dim(right_root, side_index * half_width, half_width, 1)
    partial_prod = multiply(mom_block.astype(jnp.float32), right_part)
    own_piece = multiply(left_root, partial_prod).astype(jnp.bfloat16)
    outgoing = own_piece.reshape(shards, local_rows, half_width)
    returned = lax.all_to_all(outgoing, "shard", split_axis=0, concat_axis=0, tiled=True)
    own_rows = returned.reshape(block_rows, half_cols, local_rows, half_width)
    gathered = lax.all_gather(own_rows[None], "pair", axis=0, tiled=True)
    update = (
        gathered.reshape(2, 2, block_rows, half_cols, local_rows, half_width)
        .transpose(2, 0, 3, 4, 1, 5)
        .reshape(block_rows, block_cols, local_rows, block_size)
    )
    return (update, new_momentum)


def dot(left, right, contract=((1,), (0,))):
    return lax.dot_general(
        left, right, (contract, ((), ())), preferred_element_type=jnp.float32
    )


def diagonal(rows, cols, offset):
    row = lax.broadcasted_iota(jnp.int32, (rows, cols), 0)
    col = lax.broadcasted_iota(jnp.int32, (rows, cols), 1)
    return row == col + offset


def step_kernel(
    shards,
    half_cols,
    grad,
    mom,
    update,
    grad_block,
    mom_block,
    new_block,
    left_scaled,
    left_square,
    right_scaled,
    right_square,
    right_full,
    factor,
    product,
    outgoing,
    local_sem,
    z_send,
    z_recv,
    pass_send,
    pass_recv,
    back_send,
    back_recv,
    across_send,
    across_recv,
    twin_send,
    twin_recv,
):
    rows, size = grad.shape[1:]
    half = rows // 2
    width = size // 2
    shard = lax.axis_index("shard")
    pair = lax.axis_index("pair")
    side = lax.rem(pair, 2)
    column = pair // 2
    twin = pair + 1 - 2 * side
    across = lax.rem(pair + 2, 4)

    def block_of(column_half, owner):
        return (owner // half_cols) * 2 * half_cols + column_half * half_cols + lax.rem(
            owner, half_cols
        )

    def other(step):
        return lax.rem(shard + step, shards)

    barrier = pltpu.get_barrier_semaphore()
    for step in range(1, shards):
        pl.semaphore_signal(
            barrier, inc=1, device_id={"shard": other(step)}, device_id_type=MESH
        )
    for peer in (twin, across):
        pl.semaphore_signal(barrier, inc=1, device_id={"pair": peer}, device_id_type=MESH)
    pl.semaphore_wait(barrier, shards + 1)

    def piece(owner):
        return pl.ds(pl.multiple_of(owner * rows + side * half, half), half)

    def whole_piece(owner):
        return pl.ds(pl.multiple_of(owner * rows, rows), rows)

    own_half = pl.ds(pl.multiple_of(side * half, half), half)
    sends = []
    locals_ = []
    for kind, (source, block) in enumerate(((grad, grad_block), (mom, mom_block))):
        kind_sends = []
        for step in range(1, shards):
            target = other(step)
            copy = pltpu.make_async_remote_copy(
                src_ref=source.at[block_of(column, target), own_half],
                dst_ref=block.at[piece(shard)],
                send_sem=z_send.at[kind, step - 1],
                recv_sem=z_recv.at[kind, step - 1],
                device_id={"shard": target},
                device_id_type=MESH,
            )
            copy.start()
            kind_sends.append(copy)
        sends.append(kind_sends)
        copy = pltpu.make_async_copy(
            source.at[block_of(column, shard)],
            block.at[whole_piece(shard)],
            local_sem.at[kind],
        )
        copy.start()
        locals_.append(copy)

    def collect(kind, block):
        passes = []
        for step in range(1, shards):
            sends[kind][step - 1].wait_recv()
            origin = lax.rem(shard + shards - step, shards)
            copy = pltpu.make_async_remote_copy(
                src_ref=block.at[piece(origin)],
                dst_ref=block.at[piece(origin)],
                send_sem=pass_send.at[kind, step - 1],
                recv_sem=pass_recv.at[kind, step - 1],
                device_id={"pair": twin},
                device_id_type=MESH,
            )
            copy.start()
            passes.append(copy)
        for copy in passes:
            copy.wait_recv()
        locals_[kind].wait()
        return passes

    grad_passes = collect(0, grad_block)

    values = grad_block[...]
    wide = values.astype(jnp.float32)
    total = jnp.sum(wide * wide, keepdims=True)
    scaling = 2.0 * (total / size + damping * size) / size
    inverse = 1.0 / scaling
    identity = diagonal(size, size, 0)

    def prepare(gram, scaled_ref, square_ref, full_ref):
        scaled = gram * (inverse / size) + jnp.where(identity, damping * inverse, 0.0)
        if full_ref is not None:
            full_ref[...] = scaled
        narrow = scaled.astype(jnp.bfloat16)
        scaled_ref[...] = narrow
        square_ref[...] = (
            jnp.where(identity, 0.5625, 0.0) - 0.625 * scaled + dot(narrow, narrow) / 16.0
        ).astype(jnp.bfloat16)

    prepare(dot(values, values, ((0,), (0,))), right_scaled, right_square, right_full)
    prepare(dot(values, values, ((1,), (1,))), left_scaled, left_square, None)

    def newton(first, scaled_ref, square_ref):
        second = first + dot(square_ref[...], first.astype(jnp.bfloat16))
        third = second + dot(square_ref[...], second.astype(jnp.bfloat16))
        return (first + third) * -0.3125 + dot(
            scaled_ref[...], third.astype(jnp.bfloat16)
        ) / 16.0

    own_cols = pl.ds(pl.multiple_of(side * width, width), width)
    first = right_full[:, own_cols]
    factor[...] = (
        newton(first, right_scaled, right_square)
        + jnp.where(diagonal(size, width, side * width), 0.5625, 0.0)
    ).astype(jnp.bfloat16)

    mom_passes = collect(1, mom_block)
    new_block[...] = (
        decay_rate * mom_block[...].astype(jnp.float32) + grad_block[...].astype(jnp.float32)
    ).astype(jnp.bfloat16)
    product[...] = new_block[:, own_cols].astype(jnp.float32) + dot(
        new_block[...], factor[...]
    )
    first = dot(left_scaled[...], product[...].astype(jnp.bfloat16))
    outgoing[...] = (
        (newton(first, left_scaled, left_square) + 1.5625 * product[...])
        / jnp.sqrt(scaling)
    ).astype(jnp.bfloat16)

    backs = []
    for step in range(1, shards):
        target = other(step)
        copy = pltpu.make_async_remote_copy(
            src_ref=outgoing.at[whole_piece(target)],
            dst_ref=update.at[block_of(column, shard), :, own_cols],
            send_sem=back_send.at[step - 1],
            recv_sem=back_recv.at[step - 1],
            device_id={"shard": target},
            device_id_type=MESH,
        )
        copy.start()
        backs.append(copy)
    own_copy = pltpu.make_async_copy(
        outgoing.at[whole_piece(shard)],
        update.at[block_of(column, shard), :, own_cols],
        local_sem.at[0],
    )
    own_copy.start()

    def hand_on(source, slot, owner_column, origin, send, recv, index, peer):
        copy = pltpu.make_async_remote_copy(
            src_ref=source,
            dst_ref=update.at[block_of(owner_column, origin), :, own_cols],
            send_sem=send.at[index],
            recv_sem=recv.at[index],
            device_id={"pair": peer},
            device_id_type=MESH,
        )
        copy.start()
        return copy

    acrosses = []
    twins = []
    for step in range(shards):
        origin = lax.rem(shard + shards - step, shards)
        if step:
            backs[step - 1].wait_recv()
            source = update.at[block_of(column, origin), :, own_cols]
        else:
            source = outgoing.at[whole_piece(shard)]
        acrosses.append(
            hand_on(source, None, column, origin, across_send, across_recv, step, across)
        )
        twins.append(hand_on(source, None, column, origin, twin_send, twin_recv, step, twin))
    for step in range(shards):
        origin = lax.rem(shard + shards - step, shards)
        acrosses[step].wait_recv()
        source = update.at[block_of(1 - column, origin), :, own_cols]
        twins.append(
            hand_on(
                source, None, 1 - column, origin, twin_send, twin_recv, shards + step, twin
            )
        )
    for copy in twins:
        copy.wait_recv()
    own_copy.wait()
    for copy in (
        sends[0] + sends[1] + grad_passes + mom_passes + backs + acrosses + twins
    ):
        copy.wait_send()


def by_kernel(gradient, momentum):
    new_momentum = (
        decay_rate * momentum.astype(jnp.float32) + gradient.astype(jnp.float32)
    ).astype(jnp.bfloat16)
    block_rows, block_cols, rows, size = gradient.shape
    shards = lax.axis_size("shard")
    count = block_rows * block_cols
    flat = (count, rows, size)
    width = size // 2
    vmem = pltpu.VMEM
    dma = pltpu.SemaphoreType.DMA
    update = pl.pallas_call(
        functools.partial(step_kernel, shards, block_cols // 2),
        out_shape=jax.ShapeDtypeStruct(flat, jnp.bfloat16),
        in_specs=[pl.BlockSpec(memory_space=pl.ANY)] * 2,
        out_specs=pl.BlockSpec(memory_space=pl.ANY),
        scratch_shapes=[
            vmem((size, size), jnp.bfloat16),
            vmem((size, size), jnp.bfloat16),
            vmem((size, size), jnp.bfloat16),
            vmem((size, size), jnp.bfloat16),
            vmem((size, size), jnp.bfloat16),
            vmem((size, size), jnp.bfloat16),
            vmem((size, size), jnp.bfloat16),
            vmem((size, size), jnp.float32),
            vmem((size, width), jnp.bfloat16),
            vmem((size, width), jnp.float32),
            vmem((size, width), jnp.bfloat16),
            dma((2,)),
            dma((2, shards - 1)),
            dma((2, shards - 1)),
            dma((2, shards - 1)),
            dma((2, shards - 1)),
            dma((shards - 1,)),
            dma((shards - 1,)),
            dma((shards,)),
            dma((shards,)),
            dma((2 * shards,)),
            dma((2 * shards,)),
        ],
        compiler_params=pltpu.CompilerParams(collective_id=0, has_side_effects=True),
    )(gradient.reshape(flat), momentum.reshape(flat))
    return (update.reshape(gradient.shape), new_momentum)


def local(gradient, momentum):
    block_rows, block_cols, rows, size = gradient.shape
    shards = lax.axis_size("shard")
    fits = (
        lax.axis_size("pair") == 4
        and block_rows * block_cols == 2 * shards
        and rows * shards == size
        and rows % 32 == 0
        and size % 256 == 0
    )
    return (by_kernel if fits else by_collectives)(gradient, momentum)


def solution(mesh):
    in_specs = (P("groups", None, "shard", None), P("groups", None, "shard", None))
    out_specs = (P("groups", None, "shard", None), P("groups", None, "shard", None))
    return jax.shard_map(local, mesh=mesh, in_specs=in_specs, out_specs=out_specs, check_vma=False)
```

```python
import functools

import jax
import jax.numpy as jnp
from jax import lax
from jax.experimental import pallas as pl
from jax.experimental.pallas import tpu as pltpu
from jax.sharding import PartitionSpec as P

damping = 0.1
decay_rate = 0.9
MESH = pl.DeviceIdType.MESH


def from_partner(value, axis, apart):
    mask = 2**apart
    pairs = [(source, source ^ mask) for source in range(lax.axis_size(axis))]
    return lax.ppermute(value, axis, pairs)


def multiply(left_matrix, right_matrix):
    return jnp.dot(
        left_matrix,
        right_matrix,
        precision=lax.Precision.HIGHEST,
        preferred_element_type=jnp.float32,
    )


def gram_root(gram_matrix):
    block_size = gram_matrix.shape[0]
    identity = jnp.eye(block_size, dtype=jnp.float32)
    scaling = 2.0 * jnp.trace(gram_matrix) / block_size
    root_scale = jnp.sqrt(jnp.sqrt(scaling))
    scaled = gram_matrix / scaling
    leading = (5.0 * identity - scaled) / 4.0
    iterate = leading / root_scale
    squared = multiply(leading, leading)
    fourth = multiply(squared, squared)
    shifted = multiply(fourth, scaled)
    second = (5.0 * identity - shifted) / 4.0
    return multiply(iterate, second)


def by_collectives(gradient, momentum):
    new_momentum = (
        decay_rate * momentum.astype(jnp.float32) + gradient.astype(jnp.float32)
    ).astype(jnp.bfloat16)
    block_rows, block_cols, local_rows, block_size = gradient.shape
    half_cols = block_cols // 2
    half_width = block_size // 2
    shards = lax.axis_size("shard")
    position = lax.axis_index("pair")
    column_half = position // 2
    side_index = position % 2
    leading_side = side_index == 0
    grad_half = lax.dynamic_slice_in_dim(gradient, column_half * half_cols, half_cols, 1).reshape(
        shards, local_rows, block_size
    )
    mom_half = lax.dynamic_slice_in_dim(
        new_momentum, column_half * half_cols, half_cols, 1
    ).reshape(shards, local_rows, block_size)
    grad_recv, mom_recv = (
        lax.all_to_all(grad_half, "shard", split_axis=0, concat_axis=1, tiled=True),
        lax.all_to_all(mom_half, "shard", split_axis=0, concat_axis=1, tiled=True),
    )
    grad_block = grad_recv[0]
    mom_block = mom_recv[0]
    identity = jnp.eye(block_size, dtype=jnp.float32)
    oriented = jnp.where(leading_side, grad_block, grad_block.T)
    gram_matrix = (
        jnp.dot(oriented, oriented.T, preferred_element_type=jnp.float32) / block_size
        + damping * identity
    )
    own_root = gram_root(gram_matrix)
    partner = from_partner(own_root, "pair", 0)
    left_root = jnp.where(leading_side, own_root, partner)
    right_root = jnp.where(leading_side, partner, own_root)
    right_part = lax.dynamic_slice_in_dim(right_root, side_index * half_width, half_width, 1)
    partial_prod = multiply(mom_block.astype(jnp.float32), right_part)
    own_piece = multiply(left_root, partial_prod).astype(jnp.bfloat16)
    outgoing = own_piece.reshape(shards, local_rows, half_width)
    returned = lax.all_to_all(outgoing, "shard", split_axis=0, concat_axis=0, tiled=True)
    own_rows = returned.reshape(block_rows, half_cols, local_rows, half_width)
    gathered = lax.all_gather(own_rows[None], "pair", axis=0, tiled=True)
    update = (
        gathered.reshape(2, 2, block_rows, half_cols, local_rows, half_width)
        .transpose(2, 0, 3, 4, 1, 5)
        .reshape(block_rows, block_cols, local_rows, block_size)
    )
    return (update, new_momentum)


def dot(left, right, contract=((1,), (0,))):
    return lax.dot_general(
        left, right, (contract, ((), ())), preferred_element_type=jnp.float32
    )


def diagonal(rows, cols, offset):
    row = lax.broadcasted_iota(jnp.int32, (rows, cols), 0)
    col = lax.broadcasted_iota(jnp.int32, (rows, cols), 1)
    return row == col + offset


def step_kernel(
    shards,
    half_cols,
    grad,
    mom,
    update,
    new_mom,
    grad_rows,
    mom_rows,
    grad_block,
    mom_block,
    full,
    left_scaled,
    left_square,
    right_scaled,
    right_square,
    left_factor,
    right_factor,
    product,
    outgoing,
    local_sem,
    z_send,
    z_recv,
    pass_send,
    pass_recv,
    back_send,
    back_recv,
    across_send,
    across_recv,
    twin_send,
    twin_recv,
):
    count, rows, size = grad.shape
    half = rows // 2
    width = size // 2
    shard = lax.axis_index("shard")
    pair = lax.axis_index("pair")
    side = lax.rem(pair, 2)
    column = pair // 2
    twin = pair + 1 - 2 * side
    across = lax.rem(pair + 2, 4)
    order = peer_order(shards)
    peers = []
    for mask in order:
        peer = shard
        bit = 1
        while bit < shards:
            if mask & bit:
                peer = peer + bit - 2 * bit * lax.rem(shard // bit, 2)
            bit *= 2
        peers.append(peer)

    def block_of(column_half, owner):
        return (owner // half_cols) * 2 * half_cols + column_half * half_cols + lax.rem(
            owner, half_cols
        )

    barrier = pltpu.get_barrier_semaphore()
    for peer in peers:
        pl.semaphore_signal(barrier, inc=1, device_id={"shard": peer}, device_id_type=MESH)
    for peer in (twin, across):
        pl.semaphore_signal(barrier, inc=1, device_id={"pair": peer}, device_id_type=MESH)
    loads = []
    for kind, (source, local_rows) in enumerate(((grad, grad_rows), (mom, mom_rows))):
        copy = pltpu.make_async_copy(source, local_rows, local_sem.at[kind])
        copy.start()
        loads.append(copy)
    pl.semaphore_wait(barrier, shards + 1)

    def piece(owner):
        return pl.ds(pl.multiple_of(owner * rows + side * half, half), half)

    def whole_piece(owner):
        return pl.ds(pl.multiple_of(owner * rows, rows), rows)

    own_half = pl.ds(pl.multiple_of(side * half, half), half)
    own_cols = pl.ds(pl.multiple_of(side * width, width), width)
    sends = []
    for kind, (source, block) in enumerate(((grad, grad_block), (mom, mom_block))):
        kind_sends = []
        for index, target in enumerate(peers):
            copy = pltpu.make_async_remote_copy(
                src_ref=source.at[block_of(column, target), own_half],
                dst_ref=block.at[piece(shard)],
                send_sem=z_send.at[kind, index],
                recv_sem=z_recv.at[kind, index],
                device_id={"shard": target},
                device_id_type=MESH,
            )
            copy.start()
            kind_sends.append(copy)
        sends.append(kind_sends)

    def combine(momentum, gradient):
        return (
            decay_rate * momentum.astype(jnp.float32) + gradient.astype(jnp.float32)
        ).astype(jnp.bfloat16)

    for copy in loads:
        copy.wait()
    for index in range(count):
        new_mom[index] = combine(mom_rows[index], grad_rows[index])
    grad_block[whole_piece(shard), :] = grad_rows[block_of(column, shard)]

    def collect(kind, block):
        passes = []
        for index, origin in enumerate(peers):
            sends[kind][index].wait_recv()
            copy = pltpu.make_async_remote_copy(
                src_ref=block.at[piece(origin)],
                dst_ref=block.at[piece(origin)],
                send_sem=pass_send.at[kind, index],
                recv_sem=pass_recv.at[kind, index],
                device_id={"pair": twin},
                device_id_type=MESH,
            )
            copy.start()
            passes.append(copy)
        return passes

    grad_passes = collect(0, grad_block)
    for copy in grad_passes:
        copy.wait_recv()

    values = grad_block[...]
    wide = values.astype(jnp.float32)
    total = jnp.sum(wide * wide, keepdims=True)
    scaling = 2.0 * (total / size + damping * size) / size
    inverse = 1.0 / scaling
    identity = diagonal(size, size, 0)

    def prepare(gram, scaled_ref, square_ref):
        scaled = gram * (inverse / size) + jnp.where(identity, damping * inverse, 0.0)
        full[...] = scaled
        narrow = scaled.astype(jnp.bfloat16)
        scaled_ref[...] = narrow
        square_ref[...] = (
            jnp.where(identity, 0.5625, 0.0) - 0.625 * scaled + dot(narrow, narrow) / 16.0
        ).astype(jnp.bfloat16)

    def newton(first, scaled_ref, square_ref):
        second = first + dot(square_ref[...], first.astype(jnp.bfloat16))
        third = second + dot(square_ref[...], second.astype(jnp.bfloat16))
        return (first + third) * -0.3125 + dot(
            scaled_ref[...], third.astype(jnp.bfloat16)
        ) / 16.0

    prepare(dot(values, values, ((0,), (0,))), right_scaled, right_square)
    right_factor[...] = (
        newton(full[:, own_cols], right_scaled, right_square)
        + jnp.where(diagonal(size, width, side * width), 0.5625, 0.0)
    ).astype(jnp.bfloat16)
    prepare(dot(values, values, ((1,), (1,))), left_scaled, left_square)
    left_factor[...] = (
        newton(full[...], left_scaled, left_square) + jnp.where(identity, 0.5625, 0.0)
    ).astype(jnp.bfloat16)

    def multiply_rows(new_rows, own_part, owner):
        product[whole_piece(owner), :] = own_part.astype(jnp.float32) + dot(
            new_rows, right_factor[...]
        )

    own_block = block_of(column, shard)
    multiply_rows(new_mom[own_block], new_mom[own_block, :, own_cols], shard)
    mom_passes = collect(1, mom_block)
    for copy, origin in zip(mom_passes, peers):
        copy.wait_recv()
        new_rows = combine(mom_block[whole_piece(origin), :], grad_block[whole_piece(origin), :])
        own_part = combine(
            mom_block[whole_piece(origin), own_cols], grad_block[whole_piece(origin), own_cols]
        )
        multiply_rows(new_rows, own_part, origin)

    outer = 1.0 / jnp.sqrt(scaling)
    narrow_product = product[...].astype(jnp.bfloat16)

    def update_rows(owner):
        return (
            (
                product[whole_piece(owner), :]
                + dot(left_factor[whole_piece(owner), :], narrow_product)
            )
            * outer
        ).astype(jnp.bfloat16)

    backs = []
    for index, target in enumerate(peers):
        outgoing[index] = update_rows(target)
        copy = pltpu.make_async_remote_copy(
            src_ref=outgoing.at[index],
            dst_ref=update.at[own_block, :, own_cols],
            send_sem=back_send.at[index],
            recv_sem=back_recv.at[index],
            device_id={"shard": target},
            device_id_type=MESH,
        )
        copy.start()
        backs.append(copy)
    update[own_block, :, own_cols] = update_rows(shard)

    def hand_on(block, send, recv, index, peer):
        copy = pltpu.make_async_remote_copy(
            src_ref=update.at[block, :, own_cols],
            dst_ref=update.at[block, :, own_cols],
            send_sem=send.at[index],
            recv_sem=recv.at[index],
            device_id={"pair": peer},
            device_id_type=MESH,
        )
        copy.start()
        return copy

    acrosses = []
    twins = []

    def take_across(index, origin):
        acrosses[index].wait_recv()
        twins.append(
            hand_on(block_of(1 - column, origin), twin_send, twin_recv, shards + index, twin)
        )

    origins = [shard] + peers
    for index, origin in enumerate(origins):
        if index:
            backs[index - 1].wait_recv()
        block = block_of(column, origin)
        acrosses.append(hand_on(block, across_send, across_recv, index, across))
        twins.append(hand_on(block, twin_send, twin_recv, index, twin))
        if index:
            take_across(index - 1, origins[index - 1])
    take_across(shards - 1, origins[-1])
    for copy in twins:
        copy.wait_recv()
    for copy in (
        sends[0] + sends[1] + grad_passes + mom_passes + backs + acrosses + twins
    ):
        copy.wait_send()


def peer_order(shards):
    masks = list(range(1, shards))
    return masks[:1] + masks[:0:-1]


def by_kernel(gradient, momentum):
    block_rows, block_cols, rows, size = gradient.shape
    shards = lax.axis_size("shard")
    count = block_rows * block_cols
    flat = (count, rows, size)
    width = size // 2
    vmem = pltpu.VMEM
    dma = pltpu.SemaphoreType.DMA
    square = vmem((size, size), jnp.bfloat16)
    update, new_momentum = pl.pallas_call(
        functools.partial(step_kernel, shards, block_cols // 2),
        out_shape=[pltpu.VMEM(flat, jnp.bfloat16)] * 2,
        in_specs=[pl.BlockSpec(memory_space=pl.ANY)] * 2,
        out_specs=[pl.BlockSpec(memory_space=pltpu.VMEM)] * 2,
        scratch_shapes=[
            vmem(flat, jnp.bfloat16),
            vmem(flat, jnp.bfloat16),
            square,
            square,
            vmem((size, size), jnp.float32),
            square,
            square,
            square,
            square,
            square,
            vmem((size, width), jnp.bfloat16),
            vmem((size, width), jnp.float32),
            vmem((shards - 1, rows, width), jnp.bfloat16),
            dma((2,)),
            dma((2, shards - 1)),
            dma((2, shards - 1)),
            dma((2, shards - 1)),
            dma((2, shards - 1)),
            dma((shards - 1,)),
            dma((shards - 1,)),
            dma((shards,)),
            dma((shards,)),
            dma((2 * shards,)),
            dma((2 * shards,)),
        ],
        compiler_params=pltpu.CompilerParams(collective_id=0, has_side_effects=True),
    )(gradient.reshape(flat), momentum.reshape(flat))
    return (update.reshape(gradient.shape), new_momentum.reshape(gradient.shape))


def local(gradient, momentum):
    block_rows, block_cols, rows, size = gradient.shape
    shards = lax.axis_size("shard")
    fits = (
        lax.axis_size("pair") == 4
        and block_rows * block_cols == 2 * shards
        and rows * shards == size
        and shards & (shards - 1) == 0
        and rows % 32 == 0
        and size % 256 == 0
    )
    return (by_kernel if fits else by_collectives)(gradient, momentum)


def solution(mesh):
    in_specs = (P("groups", None, "shard", None), P("groups", None, "shard", None))
    out_specs = (P("groups", None, "shard", None), P("groups", None, "shard", None))
    return jax.shard_map(local, mesh=mesh, in_specs=in_specs, out_specs=out_specs, check_vma=False)
```

```python
import functools

import jax
import jax.numpy as jnp
from jax import lax
from jax.experimental import pallas as pl
from jax.experimental.pallas import tpu as pltpu
from jax.sharding import PartitionSpec as P

damping = 0.1
decay_rate = 0.9
MESH = pl.DeviceIdType.MESH


def from_partner(value, axis, apart):
    mask = 2**apart
    pairs = [(source, source ^ mask) for source in range(lax.axis_size(axis))]
    return lax.ppermute(value, axis, pairs)


def multiply(left_matrix, right_matrix):
    return jnp.dot(
        left_matrix,
        right_matrix,
        precision=lax.Precision.HIGHEST,
        preferred_element_type=jnp.float32,
    )


def gram_root(gram_matrix):
    block_size = gram_matrix.shape[0]
    identity = jnp.eye(block_size, dtype=jnp.float32)
    scaling = 2.0 * jnp.trace(gram_matrix) / block_size
    root_scale = jnp.sqrt(jnp.sqrt(scaling))
    scaled = gram_matrix / scaling
    leading = (5.0 * identity - scaled) / 4.0
    iterate = leading / root_scale
    squared = multiply(leading, leading)
    fourth = multiply(squared, squared)
    shifted = multiply(fourth, scaled)
    second = (5.0 * identity - shifted) / 4.0
    return multiply(iterate, second)


def by_collectives(gradient, momentum):
    new_momentum = (
        decay_rate * momentum.astype(jnp.float32) + gradient.astype(jnp.float32)
    ).astype(jnp.bfloat16)
    block_rows, block_cols, local_rows, block_size = gradient.shape
    half_cols = block_cols // 2
    half_width = block_size // 2
    shards = lax.axis_size("shard")
    position = lax.axis_index("pair")
    column_half = position // 2
    side_index = position % 2
    leading_side = side_index == 0
    grad_half = lax.dynamic_slice_in_dim(gradient, column_half * half_cols, half_cols, 1).reshape(
        shards, local_rows, block_size
    )
    mom_half = lax.dynamic_slice_in_dim(
        new_momentum, column_half * half_cols, half_cols, 1
    ).reshape(shards, local_rows, block_size)
    grad_recv, mom_recv = (
        lax.all_to_all(grad_half, "shard", split_axis=0, concat_axis=1, tiled=True),
        lax.all_to_all(mom_half, "shard", split_axis=0, concat_axis=1, tiled=True),
    )
    grad_block = grad_recv[0]
    mom_block = mom_recv[0]
    identity = jnp.eye(block_size, dtype=jnp.float32)
    oriented = jnp.where(leading_side, grad_block, grad_block.T)
    gram_matrix = (
        jnp.dot(oriented, oriented.T, preferred_element_type=jnp.float32) / block_size
        + damping * identity
    )
    own_root = gram_root(gram_matrix)
    partner = from_partner(own_root, "pair", 0)
    left_root = jnp.where(leading_side, own_root, partner)
    right_root = jnp.where(leading_side, partner, own_root)
    right_part = lax.dynamic_slice_in_dim(right_root, side_index * half_width, half_width, 1)
    partial_prod = multiply(mom_block.astype(jnp.float32), right_part)
    own_piece = multiply(left_root, partial_prod).astype(jnp.bfloat16)
    outgoing = own_piece.reshape(shards, local_rows, half_width)
    returned = lax.all_to_all(outgoing, "shard", split_axis=0, concat_axis=0, tiled=True)
    own_rows = returned.reshape(block_rows, half_cols, local_rows, half_width)
    gathered = lax.all_gather(own_rows[None], "pair", axis=0, tiled=True)
    update = (
        gathered.reshape(2, 2, block_rows, half_cols, local_rows, half_width)
        .transpose(2, 0, 3, 4, 1, 5)
        .reshape(block_rows, block_cols, local_rows, block_size)
    )
    return (update, new_momentum)


def dot(left, right, contract=((1,), (0,))):
    return lax.dot_general(
        left, right, (contract, ((), ())), preferred_element_type=jnp.float32
    )


def diagonal(rows, cols, offset):
    row = lax.broadcasted_iota(jnp.int32, (rows, cols), 0)
    col = lax.broadcasted_iota(jnp.int32, (rows, cols), 1)
    return row == col + offset


def step_kernel(
    shards,
    half_cols,
    grad,
    mom,
    update,
    new_mom,
    grad_rows,
    mom_rows,
    grad_block,
    mom_block,
    full,
    power1,
    power2,
    power3,
    high,
    roots,
    product,
    outgoing,
    local_sem,
    z_send,
    z_recv,
    pass_send,
    pass_recv,
    back_send,
    back_recv,
    across_send,
    across_recv,
    twin_send,
    twin_recv,
    root_send,
    root_recv,
):
    count, rows, size = grad.shape
    half = rows // 2
    width = size // 2
    shard = lax.axis_index("shard")
    pair = lax.axis_index("pair")
    side = lax.rem(pair, 2)
    column = pair // 2
    twin = pair + 1 - 2 * side
    across = lax.rem(pair + 2, 4)
    order = peer_order(shards)
    peers = []
    for mask in order:
        peer = shard
        bit = 1
        while bit < shards:
            if mask & bit:
                peer = peer + bit - 2 * bit * lax.rem(shard // bit, 2)
            bit *= 2
        peers.append(peer)

    def block_of(column_half, owner):
        return (owner // half_cols) * 2 * half_cols + column_half * half_cols + lax.rem(
            owner, half_cols
        )

    barrier = pltpu.get_barrier_semaphore()
    for peer in peers:
        pl.semaphore_signal(barrier, inc=1, device_id={"shard": peer}, device_id_type=MESH)
    for peer in (twin, across):
        pl.semaphore_signal(barrier, inc=1, device_id={"pair": peer}, device_id_type=MESH)
    loads = []
    for kind, (source, local_rows) in enumerate(((grad, grad_rows), (mom, mom_rows))):
        copy = pltpu.make_async_copy(source, local_rows, local_sem.at[kind])
        copy.start()
        loads.append(copy)
    pl.semaphore_wait(barrier, shards + 1)

    def piece(owner):
        return pl.ds(pl.multiple_of(owner * rows + side * half, half), half)

    def whole_piece(owner):
        return pl.ds(pl.multiple_of(owner * rows, rows), rows)

    own_half = pl.ds(pl.multiple_of(side * half, half), half)
    own_cols = pl.ds(pl.multiple_of(side * width, width), width)
    sends = []
    for kind, (source, block) in enumerate(((grad, grad_block), (mom, mom_block))):
        kind_sends = []
        for index, target in enumerate(peers):
            copy = pltpu.make_async_remote_copy(
                src_ref=source.at[block_of(column, target), own_half],
                dst_ref=block.at[piece(shard)],
                send_sem=z_send.at[kind, index],
                recv_sem=z_recv.at[kind, index],
                device_id={"shard": target},
                device_id_type=MESH,
            )
            copy.start()
            kind_sends.append(copy)
        sends.append(kind_sends)

    def combine(momentum, gradient):
        return (
            decay_rate * momentum.astype(jnp.float32) + gradient.astype(jnp.float32)
        ).astype(jnp.bfloat16)

    for copy in loads:
        copy.wait()
    for index in range(count):
        new_mom[index] = combine(mom_rows[index], grad_rows[index])
    grad_block[whole_piece(shard), :] = grad_rows[block_of(column, shard)]

    def collect(kind, block):
        passes = []
        for index, origin in enumerate(peers):
            sends[kind][index].wait_recv()
            copy = pltpu.make_async_remote_copy(
                src_ref=block.at[piece(origin)],
                dst_ref=block.at[piece(origin)],
                send_sem=pass_send.at[kind, index],
                recv_sem=pass_recv.at[kind, index],
                device_id={"pair": twin},
                device_id_type=MESH,
            )
            copy.start()
            passes.append(copy)
        return passes

    grad_passes = collect(0, grad_block)
    for copy in grad_passes:
        copy.wait_recv()

    values = grad_block[...]
    wide = values.astype(jnp.float32)
    total = jnp.sum(wide * wide, keepdims=True)
    scaling = 2.0 * (total / size + damping * size) / size
    inverse = 1.0 / scaling
    identity = diagonal(size, size, 0)

    @pl.when(side == 0)
    def _():
        full[...] = dot(values, values, ((1,), (1,)))

    @pl.when(side == 1)
    def _():
        full[...] = dot(values, values, ((0,), (0,)))

    shifted = full[...] * (inverse / size) + jnp.where(identity, damping * inverse - 1.0, 0.0)
    full[...] = shifted
    power1[...] = shifted.astype(jnp.bfloat16)
    squared = dot(power1[...], power1[...])
    power2[...] = squared.astype(jnp.bfloat16)
    cubed = dot(power2[...], power1[...])
    power3[...] = cubed.astype(jnp.bfloat16)
    high[...] = (
        (35 / 1024) * full[...]
        + (-19 / 4096) * squared
        + (1 / 4096) * cubed
        - jnp.where(identity, 15 / 128, 0.0)
    ).astype(jnp.bfloat16)
    full[...] = (5 / 32) * squared - 0.25 * full[...]
    root_copies = []
    for index in range(2):
        part = pl.ds(index * width, width)
        roots[side, part, :] = (full[part, :] + dot(power3[part, :], high[...])).astype(
            jnp.bfloat16
        )
        copy = pltpu.make_async_remote_copy(
            src_ref=roots.at[side, part],
            dst_ref=roots.at[side, part],
            send_sem=root_send.at[index],
            recv_sem=root_recv.at[index],
            device_id={"pair": twin},
            device_id_type=MESH,
        )
        copy.start()
        root_copies.append(copy)

    def multiply_rows(new_rows, own_part, owner):
        product[whole_piece(owner), :] = own_part.astype(jnp.float32) + dot(
            new_rows, roots[1, :, own_cols]
        )

    own_block = block_of(column, shard)
    mom_passes = collect(1, mom_block)
    for copy in root_copies:
        copy.wait_recv()
    multiply_rows(new_mom[own_block], new_mom[own_block, :, own_cols], shard)
    for copy, origin in zip(mom_passes, peers):
        copy.wait_recv()
        new_rows = combine(mom_block[whole_piece(origin), :], grad_block[whole_piece(origin), :])
        own_part = combine(
            mom_block[whole_piece(origin), own_cols], grad_block[whole_piece(origin), own_cols]
        )
        multiply_rows(new_rows, own_part, origin)

    outer = 1.0 / jnp.sqrt(scaling)
    narrow_product = product[...].astype(jnp.bfloat16)

    def update_rows(owner):
        return (
            (
                product[whole_piece(owner), :]
                + dot(roots[0, whole_piece(owner), :], narrow_product)
            )
            * outer
        ).astype(jnp.bfloat16)

    def part_rows(part):
        return pl.ds(part * half, half)

    backs = []
    for index, target in enumerate(peers):
        outgoing[index] = update_rows(target)
        for part in range(2):
            copy = pltpu.make_async_remote_copy(
                src_ref=outgoing.at[index, part_rows(part)],
                dst_ref=update.at[own_block, part_rows(part), own_cols],
                send_sem=back_send.at[2 * index + part],
                recv_sem=back_recv.at[2 * index + part],
                device_id={"shard": target},
                device_id_type=MESH,
            )
            copy.start()
            backs.append(copy)
    update[own_block, :, own_cols] = update_rows(shard)

    def hand_on(block, part, send, recv, index, peer):
        copy = pltpu.make_async_remote_copy(
            src_ref=update.at[block, part_rows(part), own_cols],
            dst_ref=update.at[block, part_rows(part), own_cols],
            send_sem=send.at[index],
            recv_sem=recv.at[index],
            device_id={"pair": peer},
            device_id_type=MESH,
        )
        copy.start()
        return copy

    origins = [shard] + peers
    acrosses = []
    twins = []

    def take_across(index):
        acrosses[index].wait_recv()
        block = block_of(1 - column, origins[index // 2])
        twins.append(
            hand_on(block, index % 2, twin_send, twin_recv, 2 * shards + index, twin)
        )

    for index in range(2 * shards):
        if index >= 2:
            backs[index - 2].wait_recv()
        block = block_of(column, origins[index // 2])
        acrosses.append(hand_on(block, index % 2, across_send, across_recv, index, across))
        twins.append(hand_on(block, index % 2, twin_send, twin_recv, index, twin))
        if index >= 2:
            take_across(index - 2)
    take_across(2 * shards - 2)
    take_across(2 * shards - 1)
    for copy in twins:
        copy.wait_recv()
    for copy in (
        sends[0]
        + sends[1]
        + grad_passes
        + mom_passes
        + root_copies
        + backs
        + acrosses
        + twins
    ):
        copy.wait_send()


def store_kernel(parts, update, new_mom, update_out, new_mom_out, sems):
    size = update.shape[0] // parts
    copies = []
    for kind, (source, target) in enumerate(((update, update_out), (new_mom, new_mom_out))):
        for part in range(parts):
            piece = pl.ds(part * size, size)
            copy = pltpu.make_async_copy(
                source.at[piece], target.at[piece], sems.at[kind, part]
            )
            copy.start()
            copies.append(copy)
    for copy in copies:
        copy.wait()


def peer_order(shards):
    masks = list(range(1, shards))
    return masks[:1] + masks[:0:-1]


def by_kernel(gradient, momentum):
    block_rows, block_cols, rows, size = gradient.shape
    shards = lax.axis_size("shard")
    count = block_rows * block_cols
    flat = (count, rows, size)
    width = size // 2
    vmem = pltpu.VMEM
    dma = pltpu.SemaphoreType.DMA
    square = vmem((size, size), jnp.bfloat16)
    update, new_momentum = pl.pallas_call(
        functools.partial(step_kernel, shards, block_cols // 2),
        out_shape=[pltpu.VMEM(flat, jnp.bfloat16)] * 2,
        in_specs=[pl.BlockSpec(memory_space=pl.ANY)] * 2,
        out_specs=[pl.BlockSpec(memory_space=pltpu.VMEM)] * 2,
        scratch_shapes=[
            vmem(flat, jnp.bfloat16),
            vmem(flat, jnp.bfloat16),
            square,
            square,
            vmem((size, size), jnp.float32),
            square,
            square,
            square,
            square,
            vmem((2, size, size), jnp.bfloat16),
            vmem((size, width), jnp.float32),
            vmem((shards - 1, rows, width), jnp.bfloat16),
            dma((2,)),
            dma((2, shards - 1)),
            dma((2, shards - 1)),
            dma((2, shards - 1)),
            dma((2, shards - 1)),
            dma((2 * shards - 2,)),
            dma((2 * shards - 2,)),
            dma((2 * shards,)),
            dma((2 * shards,)),
            dma((4 * shards,)),
            dma((4 * shards,)),
            dma((2,)),
            dma((2,)),
        ],
        compiler_params=pltpu.CompilerParams(collective_id=0, has_side_effects=True),
    )(gradient.reshape(flat), momentum.reshape(flat))
    update, new_momentum = pl.pallas_call(
        functools.partial(store_kernel, 4),
        out_shape=[jax.ShapeDtypeStruct(flat, jnp.bfloat16)] * 2,
        in_specs=[pl.BlockSpec(memory_space=pl.ANY)] * 2,
        out_specs=[pl.BlockSpec(memory_space=pl.ANY)] * 2,
        scratch_shapes=[dma((2, 4))],
    )(update, new_momentum)
    return (update.reshape(gradient.shape), new_momentum.reshape(gradient.shape))


def local(gradient, momentum):
    block_rows, block_cols, rows, size = gradient.shape
    shards = lax.axis_size("shard")
    fits = (
        lax.axis_size("pair") == 4
        and block_rows * block_cols == 2 * shards
        and rows * shards == size
        and shards & (shards - 1) == 0
        and rows % 32 == 0
        and size % 256 == 0
    )
    return (by_kernel if fits else by_collectives)(gradient, momentum)


def solution(mesh):
    in_specs = (P("groups", None, "shard", None), P("groups", None, "shard", None))
    out_specs = (P("groups", None, "shard", None), P("groups", None, "shard", None))
    return jax.shard_map(local, mesh=mesh, in_specs=in_specs, out_specs=out_specs, check_vma=False)
```

```python
import functools

import jax
import jax.numpy as jnp
from jax import lax
from jax.experimental import pallas as pl
from jax.experimental.pallas import tpu as pltpu
from jax.sharding import PartitionSpec as P

damping = 0.1
decay_rate = 0.9
MESH = pl.DeviceIdType.MESH


def from_partner(value, axis, apart):
    mask = 2**apart
    pairs = [(source, source ^ mask) for source in range(lax.axis_size(axis))]
    return lax.ppermute(value, axis, pairs)


def multiply(left_matrix, right_matrix):
    return jnp.dot(
        left_matrix,
        right_matrix,
        precision=lax.Precision.HIGHEST,
        preferred_element_type=jnp.float32,
    )


def gram_root(gram_matrix):
    block_size = gram_matrix.shape[0]
    identity = jnp.eye(block_size, dtype=jnp.float32)
    scaling = 2.0 * jnp.trace(gram_matrix) / block_size
    root_scale = jnp.sqrt(jnp.sqrt(scaling))
    scaled = gram_matrix / scaling
    leading = (5.0 * identity - scaled) / 4.0
    iterate = leading / root_scale
    squared = multiply(leading, leading)
    fourth = multiply(squared, squared)
    shifted = multiply(fourth, scaled)
    second = (5.0 * identity - shifted) / 4.0
    return multiply(iterate, second)


def by_collectives(gradient, momentum):
    new_momentum = (
        decay_rate * momentum.astype(jnp.float32) + gradient.astype(jnp.float32)
    ).astype(jnp.bfloat16)
    block_rows, block_cols, local_rows, block_size = gradient.shape
    half_cols = block_cols // 2
    half_width = block_size // 2
    shards = lax.axis_size("shard")
    position = lax.axis_index("pair")
    column_half = position // 2
    side_index = position % 2
    leading_side = side_index == 0
    grad_half = lax.dynamic_slice_in_dim(gradient, column_half * half_cols, half_cols, 1).reshape(
        shards, local_rows, block_size
    )
    mom_half = lax.dynamic_slice_in_dim(
        new_momentum, column_half * half_cols, half_cols, 1
    ).reshape(shards, local_rows, block_size)
    grad_recv, mom_recv = (
        lax.all_to_all(grad_half, "shard", split_axis=0, concat_axis=1, tiled=True),
        lax.all_to_all(mom_half, "shard", split_axis=0, concat_axis=1, tiled=True),
    )
    grad_block = grad_recv[0]
    mom_block = mom_recv[0]
    identity = jnp.eye(block_size, dtype=jnp.float32)
    oriented = jnp.where(leading_side, grad_block, grad_block.T)
    gram_matrix = (
        jnp.dot(oriented, oriented.T, preferred_element_type=jnp.float32) / block_size
        + damping * identity
    )
    own_root = gram_root(gram_matrix)
    partner = from_partner(own_root, "pair", 0)
    left_root = jnp.where(leading_side, own_root, partner)
    right_root = jnp.where(leading_side, partner, own_root)
    right_part = lax.dynamic_slice_in_dim(right_root, side_index * half_width, half_width, 1)
    partial_prod = multiply(mom_block.astype(jnp.float32), right_part)
    own_piece = multiply(left_root, partial_prod).astype(jnp.bfloat16)
    outgoing = own_piece.reshape(shards, local_rows, half_width)
    returned = lax.all_to_all(outgoing, "shard", split_axis=0, concat_axis=0, tiled=True)
    own_rows = returned.reshape(block_rows, half_cols, local_rows, half_width)
    gathered = lax.all_gather(own_rows[None], "pair", axis=0, tiled=True)
    update = (
        gathered.reshape(2, 2, block_rows, half_cols, local_rows, half_width)
        .transpose(2, 0, 3, 4, 1, 5)
        .reshape(block_rows, block_cols, local_rows, block_size)
    )
    return (update, new_momentum)


def dot(left, right, contract=((1,), (0,))):
    return lax.dot_general(
        left, right, (contract, ((), ())), preferred_element_type=jnp.float32
    )


def diagonal(rows, cols, offset):
    row = lax.broadcasted_iota(jnp.int32, (rows, cols), 0)
    col = lax.broadcasted_iota(jnp.int32, (rows, cols), 1)
    return row == col + offset


def step_kernel(
    shards,
    half_cols,
    grad,
    mom,
    update,
    new_mom,
    grad_rows,
    mom_rows,
    grad_block,
    mom_block,
    full,
    power1,
    power2,
    power3,
    high,
    roots,
    product,
    outgoing,
    local_sem,
    z_send,
    z_recv,
    pass_send,
    pass_recv,
    back_send,
    back_recv,
    across_send,
    across_recv,
    twin_send,
    twin_recv,
    root_send,
    root_recv,
):
    count, rows, size = grad.shape
    half = rows // 2
    width = size // 2
    shard = lax.axis_index("shard")
    pair = lax.axis_index("pair")
    side = lax.rem(pair, 2)
    column = pair // 2
    twin = pair + 1 - 2 * side
    across = lax.rem(pair + 2, 4)
    order = peer_order(shards)
    peers = []
    for mask in order:
        peer = shard
        bit = 1
        while bit < shards:
            if mask & bit:
                peer = peer + bit - 2 * bit * lax.rem(shard // bit, 2)
            bit *= 2
        peers.append(peer)

    def block_of(column_half, owner):
        return (owner // half_cols) * 2 * half_cols + column_half * half_cols + lax.rem(
            owner, half_cols
        )

    barrier = pltpu.get_barrier_semaphore()
    for peer in peers:
        pl.semaphore_signal(barrier, inc=1, device_id={"shard": peer}, device_id_type=MESH)
    for peer in (twin, across):
        pl.semaphore_signal(barrier, inc=1, device_id={"pair": peer}, device_id_type=MESH)
    loads = []
    for kind, (source, local_rows) in enumerate(((grad, grad_rows), (mom, mom_rows))):
        copy = pltpu.make_async_copy(source, local_rows, local_sem.at[kind])
        copy.start()
        loads.append(copy)
    pl.semaphore_wait(barrier, shards + 1)

    def piece(owner):
        return pl.ds(pl.multiple_of(owner * rows + side * half, half), half)

    def whole_piece(owner):
        return pl.ds(pl.multiple_of(owner * rows, rows), rows)

    own_half = pl.ds(pl.multiple_of(side * half, half), half)
    own_cols = pl.ds(pl.multiple_of(side * width, width), width)
    sends = []
    for kind, (source, block) in enumerate(((grad, grad_block), (mom, mom_block))):
        kind_sends = []
        for index, target in enumerate(peers):
            copy = pltpu.make_async_remote_copy(
                src_ref=source.at[block_of(column, target), own_half],
                dst_ref=block.at[piece(shard)],
                send_sem=z_send.at[kind, index],
                recv_sem=z_recv.at[kind, index],
                device_id={"shard": target},
                device_id_type=MESH,
            )
            copy.start()
            kind_sends.append(copy)
        sends.append(kind_sends)

    def combine(momentum, gradient):
        return (
            decay_rate * momentum.astype(jnp.float32) + gradient.astype(jnp.float32)
        ).astype(jnp.bfloat16)

    for copy in loads:
        copy.wait()
    for index in range(count):
        new_mom[index] = combine(mom_rows[index], grad_rows[index])
    grad_block[whole_piece(shard), :] = grad_rows[block_of(column, shard)]

    def collect(kind, block):
        passes = []
        for index, origin in enumerate(peers):
            sends[kind][index].wait_recv()
            copy = pltpu.make_async_remote_copy(
                src_ref=block.at[piece(origin)],
                dst_ref=block.at[piece(origin)],
                send_sem=pass_send.at[kind, index],
                recv_sem=pass_recv.at[kind, index],
                device_id={"pair": twin},
                device_id_type=MESH,
            )
            copy.start()
            passes.append(copy)
        return passes

    grad_passes = collect(0, grad_block)
    for copy in grad_passes:
        copy.wait_recv()

    values = grad_block[...]
    wide = values.astype(jnp.float32)
    total = jnp.sum(wide * wide, keepdims=True)
    scaling = 2.0 * (total / size + damping * size) / size
    inverse = 1.0 / scaling
    identity = diagonal(size, size, 0)

    @pl.when(side == 0)
    def _():
        full[...] = dot(values, values, ((1,), (1,)))

    @pl.when(side == 1)
    def _():
        full[...] = dot(values, values, ((0,), (0,)))

    shifted = full[...] * (inverse / size) + jnp.where(identity, damping * inverse - 1.0, 0.0)
    full[...] = shifted
    power1[...] = shifted.astype(jnp.bfloat16)
    squared = dot(power1[...], power1[...])
    power2[...] = squared.astype(jnp.bfloat16)
    cubed = dot(power2[...], power1[...])
    power3[...] = cubed.astype(jnp.bfloat16)
    high[...] = (
        (35 / 1024) * full[...]
        + (-19 / 4096) * squared
        + (1 / 4096) * cubed
        - jnp.where(identity, 15 / 128, 0.0)
    ).astype(jnp.bfloat16)
    full[...] = (5 / 32) * squared - 0.25 * full[...]
    root_copies = []
    for index in range(2):
        part = pl.ds(index * width, width)
        roots[side, part, :] = (full[part, :] + dot(power3[part, :], high[...])).astype(
            jnp.bfloat16
        )
        copy = pltpu.make_async_remote_copy(
            src_ref=roots.at[side, part],
            dst_ref=roots.at[side, part],
            send_sem=root_send.at[index],
            recv_sem=root_recv.at[index],
            device_id={"pair": twin},
            device_id_type=MESH,
        )
        copy.start()
        root_copies.append(copy)

    def multiply_rows(new_rows, own_part, owner):
        product[whole_piece(owner), :] = own_part.astype(jnp.float32) + dot(
            new_rows, roots[1, :, own_cols]
        )

    own_block = block_of(column, shard)
    mom_passes = collect(1, mom_block)
    for copy in root_copies:
        copy.wait_recv()
    multiply_rows(new_mom[own_block], new_mom[own_block, :, own_cols], shard)
    for copy, origin in zip(mom_passes, peers):
        copy.wait_recv()
        new_rows = combine(mom_block[whole_piece(origin), :], grad_block[whole_piece(origin), :])
        own_part = combine(
            mom_block[whole_piece(origin), own_cols], grad_block[whole_piece(origin), own_cols]
        )
        multiply_rows(new_rows, own_part, origin)

    outer = 1.0 / jnp.sqrt(scaling)
    narrow_product = product[...].astype(jnp.bfloat16)

    def update_rows(owner):
        return (
            (
                product[whole_piece(owner), :]
                + dot(roots[0, whole_piece(owner), :], narrow_product)
            )
            * outer
        ).astype(jnp.bfloat16)

    def part_rows(part):
        return pl.ds(part * half, half)

    backs = []
    for index, target in enumerate(peers):
        outgoing[index] = update_rows(target)
        for part in range(2):
            copy = pltpu.make_async_remote_copy(
                src_ref=outgoing.at[index, part_rows(part)],
                dst_ref=update.at[own_block, part_rows(part), own_cols],
                send_sem=back_send.at[2 * index + part],
                recv_sem=back_recv.at[2 * index + part],
                device_id={"shard": target},
                device_id_type=MESH,
            )
            copy.start()
            backs.append(copy)
    update[own_block, :, own_cols] = update_rows(shard)

    def hand_on(block, part, send, recv, index, peer):
        copy = pltpu.make_async_remote_copy(
            src_ref=update.at[block, part_rows(part), own_cols],
            dst_ref=update.at[block, part_rows(part), own_cols],
            send_sem=send.at[index],
            recv_sem=recv.at[index],
            device_id={"pair": peer},
            device_id_type=MESH,
        )
        copy.start()
        return copy

    origins = [shard] + peers
    acrosses = []
    twins = []

    def take_across(index):
        acrosses[index].wait_recv()
        block = block_of(1 - column, origins[index // 2])
        twins.append(
            hand_on(block, index % 2, twin_send, twin_recv, 2 * shards + index, twin)
        )

    for index in range(2 * shards):
        if index >= 2:
            backs[index - 2].wait_recv()
        block = block_of(column, origins[index // 2])
        acrosses.append(hand_on(block, index % 2, across_send, across_recv, index, across))
        twins.append(hand_on(block, index % 2, twin_send, twin_recv, index, twin))
        if index >= 2:
            take_across(index - 2)
    take_across(2 * shards - 2)
    take_across(2 * shards - 1)
    for copy in twins:
        copy.wait_recv()
    for copy in (
        sends[0]
        + sends[1]
        + grad_passes
        + mom_passes
        + root_copies
        + backs
        + acrosses
        + twins
    ):
        copy.wait_send()


def peer_order(shards):
    masks = list(range(1, shards))
    return masks[:1] + masks[:0:-1]


def by_kernel(gradient, momentum):
    block_rows, block_cols, rows, size = gradient.shape
    shards = lax.axis_size("shard")
    count = block_rows * block_cols
    flat = (count, rows, size)
    width = size // 2
    vmem = pltpu.VMEM
    dma = pltpu.SemaphoreType.DMA
    square = vmem((size, size), jnp.bfloat16)
    update, new_momentum = pl.pallas_call(
        functools.partial(step_kernel, shards, block_cols // 2),
        out_shape=[pltpu.VMEM(flat, jnp.bfloat16)] * 2,
        in_specs=[pl.BlockSpec(memory_space=pl.ANY)] * 2,
        out_specs=[pl.BlockSpec(memory_space=pltpu.VMEM)] * 2,
        scratch_shapes=[
            vmem(flat, jnp.bfloat16),
            vmem(flat, jnp.bfloat16),
            square,
            square,
            vmem((size, size), jnp.float32),
            square,
            square,
            square,
            square,
            vmem((2, size, size), jnp.bfloat16),
            vmem((size, width), jnp.float32),
            vmem((shards - 1, rows, width), jnp.bfloat16),
            dma((2,)),
            dma((2, shards - 1)),
            dma((2, shards - 1)),
            dma((2, shards - 1)),
            dma((2, shards - 1)),
            dma((2 * shards - 2,)),
            dma((2 * shards - 2,)),
            dma((2 * shards,)),
            dma((2 * shards,)),
            dma((4 * shards,)),
            dma((4 * shards,)),
            dma((2,)),
            dma((2,)),
        ],
        compiler_params=pltpu.CompilerParams(collective_id=0, has_side_effects=True),
    )(gradient.reshape(flat), momentum.reshape(flat))
    return (update.reshape(gradient.shape), new_momentum.reshape(gradient.shape))


def local(gradient, momentum):
    block_rows, block_cols, rows, size = gradient.shape
    shards = lax.axis_size("shard")
    fits = (
        lax.axis_size("pair") == 4
        and block_rows * block_cols == 2 * shards
        and rows * shards == size
        and shards & (shards - 1) == 0
        and rows % 32 == 0
        and size % 256 == 0
    )
    return (by_kernel if fits else by_collectives)(gradient, momentum)


def solution(mesh):
    in_specs = (P("groups", None, "shard", None), P("groups", None, "shard", None))
    out_specs = (P("groups", None, "shard", None), P("groups", None, "shard", None))
    return jax.shard_map(local, mesh=mesh, in_specs=in_specs, out_specs=out_specs, check_vma=False)
```

```python
import functools

import jax
import jax.numpy as jnp
from jax import lax
from jax.experimental import pallas as pl
from jax.experimental.pallas import tpu as pltpu
from jax.sharding import PartitionSpec as P

damping = 0.1
decay_rate = 0.9
MESH = pl.DeviceIdType.MESH


def from_partner(value, axis, apart):
    mask = 2**apart
    pairs = [(source, source ^ mask) for source in range(lax.axis_size(axis))]
    return lax.ppermute(value, axis, pairs)


def multiply(left_matrix, right_matrix):
    return jnp.dot(
        left_matrix,
        right_matrix,
        precision=lax.Precision.HIGHEST,
        preferred_element_type=jnp.float32,
    )


def gram_root(gram_matrix):
    block_size = gram_matrix.shape[0]
    identity = jnp.eye(block_size, dtype=jnp.float32)
    scaling = 2.0 * jnp.trace(gram_matrix) / block_size
    root_scale = jnp.sqrt(jnp.sqrt(scaling))
    scaled = gram_matrix / scaling
    leading = (5.0 * identity - scaled) / 4.0
    iterate = leading / root_scale
    squared = multiply(leading, leading)
    fourth = multiply(squared, squared)
    shifted = multiply(fourth, scaled)
    second = (5.0 * identity - shifted) / 4.0
    return multiply(iterate, second)


def by_collectives(gradient, momentum):
    new_momentum = (
        decay_rate * momentum.astype(jnp.float32) + gradient.astype(jnp.float32)
    ).astype(jnp.bfloat16)
    block_rows, block_cols, local_rows, block_size = gradient.shape
    half_cols = block_cols // 2
    half_width = block_size // 2
    shards = lax.axis_size("shard")
    position = lax.axis_index("pair")
    column_half = position // 2
    side_index = position % 2
    leading_side = side_index == 0
    grad_half = lax.dynamic_slice_in_dim(gradient, column_half * half_cols, half_cols, 1).reshape(
        shards, local_rows, block_size
    )
    mom_half = lax.dynamic_slice_in_dim(
        new_momentum, column_half * half_cols, half_cols, 1
    ).reshape(shards, local_rows, block_size)
    grad_recv, mom_recv = (
        lax.all_to_all(grad_half, "shard", split_axis=0, concat_axis=1, tiled=True),
        lax.all_to_all(mom_half, "shard", split_axis=0, concat_axis=1, tiled=True),
    )
    grad_block = grad_recv[0]
    mom_block = mom_recv[0]
    identity = jnp.eye(block_size, dtype=jnp.float32)
    oriented = jnp.where(leading_side, grad_block, grad_block.T)
    gram_matrix = (
        jnp.dot(oriented, oriented.T, preferred_element_type=jnp.float32) / block_size
        + damping * identity
    )
    own_root = gram_root(gram_matrix)
    partner = from_partner(own_root, "pair", 0)
    left_root = jnp.where(leading_side, own_root, partner)
    right_root = jnp.where(leading_side, partner, own_root)
    right_part = lax.dynamic_slice_in_dim(right_root, side_index * half_width, half_width, 1)
    partial_prod = multiply(mom_block.astype(jnp.float32), right_part)
    own_piece = multiply(left_root, partial_prod).astype(jnp.bfloat16)
    outgoing = own_piece.reshape(shards, local_rows, half_width)
    returned = lax.all_to_all(outgoing, "shard", split_axis=0, concat_axis=0, tiled=True)
    own_rows = returned.reshape(block_rows, half_cols, local_rows, half_width)
    gathered = lax.all_gather(own_rows[None], "pair", axis=0, tiled=True)
    update = (
        gathered.reshape(2, 2, block_rows, half_cols, local_rows, half_width)
        .transpose(2, 0, 3, 4, 1, 5)
        .reshape(block_rows, block_cols, local_rows, block_size)
    )
    return (update, new_momentum)


def dot(left, right, contract=((1,), (0,))):
    return lax.dot_general(
        left, right, (contract, ((), ())), preferred_element_type=jnp.float32
    )


def diagonal(rows, cols, offset):
    row = lax.broadcasted_iota(jnp.int32, (rows, cols), 0)
    col = lax.broadcasted_iota(jnp.int32, (rows, cols), 1)
    return row == col + offset


def step_kernel(
    shards,
    half_cols,
    grad,
    mom,
    update,
    new_mom,
    grad_rows,
    mom_rows,
    grad_block,
    mom_block,
    full,
    power1,
    power2,
    power3,
    high,
    roots,
    product,
    outgoing,
    local_sem,
    z_send,
    z_recv,
    pass_send,
    pass_recv,
    back_send,
    back_recv,
    across_send,
    across_recv,
    twin_send,
    twin_recv,
    root_send,
    root_recv,
    seen,
):
    count, rows, size = grad.shape
    half = rows // 2
    width = size // 2
    shard = lax.axis_index("shard")
    pair = lax.axis_index("pair")
    side = lax.rem(pair, 2)
    column = pair // 2
    twin = pair + 1 - 2 * side
    across = lax.rem(pair + 2, 4)
    last = shards - 1
    lower = 1 - shard // (shards // 2)
    place = lower * shard + (1 - lower) * (last - shard)
    peers = []
    for step in range(last):
        mirrored = step + (step - place + shards) // shards
        peers.append(lower * mirrored + (1 - lower) * (last - mirrored))

    def block_of(column_half, owner):
        return (owner // half_cols) * 2 * half_cols + column_half * half_cols + lax.rem(
            owner, half_cols
        )

    barrier = pltpu.get_barrier_semaphore()

    def greet(semaphore, peer):
        pl.semaphore_signal(semaphore, inc=1, device_id={"shard": peer}, device_id_type=MESH)

    @pl.when(shard > 0)
    def _():
        greet(barrier, shard - 1)

    @pl.when(shard < last)
    def _():
        greet(barrier, shard + 1)

    for peer in (twin, across):
        pl.semaphore_signal(barrier, inc=1, device_id={"pair": peer}, device_id_type=MESH)
    loads = []
    for kind, (source, local_rows) in enumerate(((grad, grad_rows), (mom, mom_rows))):
        copy = pltpu.make_async_copy(source, local_rows, local_sem.at[kind])
        copy.start()
        loads.append(copy)
    pl.semaphore_wait(barrier, 2 + (shard + last) // shards + (2 * last - shard) // shards)

    def piece(owner):
        return pl.ds(pl.multiple_of(owner * rows + side * half, half), half)

    def whole_piece(owner):
        return pl.ds(pl.multiple_of(owner * rows, rows), rows)

    own_half = pl.ds(pl.multiple_of(side * half, half), half)
    own_cols = pl.ds(pl.multiple_of(side * width, width), width)
    def row_copy(kind, target, origin):
        source, block = ((grad, grad_block), (mom, mom_block))[kind]
        return pltpu.make_async_remote_copy(
            src_ref=source.at[block_of(column, target), own_half],
            dst_ref=block.at[piece(origin)],
            send_sem=z_send.at[kind, target],
            recv_sem=z_recv.at[kind, origin],
            device_id={"shard": target},
            device_id_type=MESH,
        )

    for distance in range(1, shards):
        if distance > 1:

            @pl.when(shard >= distance - 1)
            def _():
                @pl.when(shard < last)
                def _():
                    greet(seen.at[0, distance - 2], shard + 1)

            @pl.when(shard <= last - (distance - 1))
            def _():
                @pl.when(shard > 0)
                def _():
                    greet(seen.at[1, distance - 2], shard - 1)

        @pl.when(shard <= last - distance)
        def _():
            if distance > 1:
                pl.semaphore_wait(seen.at[1, distance - 2], 1)
            row_copy(0, shard + distance, shard).start()

        @pl.when(shard >= distance)
        def _():
            if distance > 1:
                pl.semaphore_wait(seen.at[0, distance - 2], 1)
            row_copy(0, shard - distance, shard).start()

    sends = [row_copy(0, target, shard) for target in peers]
    for target in peers:
        copy = row_copy(1, target, shard)
        copy.start()
        sends.append(copy)

    def combine(momentum, gradient):
        return (
            decay_rate * momentum.astype(jnp.float32) + gradient.astype(jnp.float32)
        ).astype(jnp.bfloat16)

    for copy in loads:
        copy.wait()
    for index in range(count):
        new_mom[index] = combine(mom_rows[index], grad_rows[index])
    grad_block[whole_piece(shard), :] = grad_rows[block_of(column, shard)]

    def collect(kind, block):
        passes = []
        for index, origin in enumerate(peers):
            row_copy(kind, shard, origin).wait_recv()
            copy = pltpu.make_async_remote_copy(
                src_ref=block.at[piece(origin)],
                dst_ref=block.at[piece(origin)],
                send_sem=pass_send.at[kind, index],
                recv_sem=pass_recv.at[kind, index],
                device_id={"pair": twin},
                device_id_type=MESH,
            )
            copy.start()
            passes.append(copy)
        return passes

    grad_passes = collect(0, grad_block)
    for copy in grad_passes:
        copy.wait_recv()

    values = grad_block[...]
    wide = values.astype(jnp.float32)
    total = jnp.sum(wide * wide, keepdims=True)
    scaling = 2.0 * (total / size + damping * size) / size
    inverse = 1.0 / scaling
    identity = diagonal(size, size, 0)

    @pl.when(side == 0)
    def _():
        full[...] = dot(values, values, ((1,), (1,)))

    @pl.when(side == 1)
    def _():
        full[...] = dot(values, values, ((0,), (0,)))

    shifted = full[...] * (inverse / size) + jnp.where(identity, damping * inverse - 1.0, 0.0)
    full[...] = shifted
    power1[...] = shifted.astype(jnp.bfloat16)
    squared = dot(power1[...], power1[...])
    power2[...] = squared.astype(jnp.bfloat16)
    cubed = dot(power2[...], power1[...])
    power3[...] = cubed.astype(jnp.bfloat16)
    high[...] = (
        (35 / 1024) * full[...]
        + (-19 / 4096) * squared
        + (1 / 4096) * cubed
        - jnp.where(identity, 15 / 128, 0.0)
    ).astype(jnp.bfloat16)
    full[...] = (5 / 32) * squared - 0.25 * full[...]
    root_copies = []
    for index in range(2):
        part = pl.ds(index * width, width)
        roots[side, part, :] = (full[part, :] + dot(power3[part, :], high[...])).astype(
            jnp.bfloat16
        )
        copy = pltpu.make_async_remote_copy(
            src_ref=roots.at[side, part],
            dst_ref=roots.at[side, part],
            send_sem=root_send.at[index],
            recv_sem=root_recv.at[index],
            device_id={"pair": twin},
            device_id_type=MESH,
        )
        copy.start()
        root_copies.append(copy)

    def multiply_rows(new_rows, own_part, owner):
        product[whole_piece(owner), :] = own_part.astype(jnp.float32) + dot(
            new_rows, roots[1, :, own_cols]
        )

    own_block = block_of(column, shard)
    mom_passes = collect(1, mom_block)
    for copy in root_copies:
        copy.wait_recv()
    multiply_rows(new_mom[own_block], new_mom[own_block, :, own_cols], shard)
    for copy, origin in zip(mom_passes, peers):
        copy.wait_recv()
        new_rows = combine(mom_block[whole_piece(origin), :], grad_block[whole_piece(origin), :])
        own_part = combine(
            mom_block[whole_piece(origin), own_cols], grad_block[whole_piece(origin), own_cols]
        )
        multiply_rows(new_rows, own_part, origin)

    outer = 1.0 / jnp.sqrt(scaling)
    narrow_product = product[...].astype(jnp.bfloat16)

    def update_rows(owner):
        return (
            (
                product[whole_piece(owner), :]
                + dot(roots[0, whole_piece(owner), :], narrow_product)
            )
            * outer
        ).astype(jnp.bfloat16)

    def back_copy(index, target, origin):
        return pltpu.make_async_remote_copy(
            src_ref=outgoing.at[index],
            dst_ref=update.at[block_of(column, origin), :, own_cols],
            send_sem=back_send.at[index],
            recv_sem=back_recv.at[origin],
            device_id={"shard": target},
            device_id_type=MESH,
        )

    backs = []
    for index, target in enumerate(peers):
        outgoing[index] = update_rows(target)
        copy = back_copy(index, target, shard)
        copy.start()
        backs.append(copy)
    update[own_block, :, own_cols] = update_rows(shard)

    def hand_on(block, send, recv, index, peer):
        copy = pltpu.make_async_remote_copy(
            src_ref=update.at[block, :, own_cols],
            dst_ref=update.at[block, :, own_cols],
            send_sem=send.at[index],
            recv_sem=recv.at[index],
            device_id={"pair": peer},
            device_id_type=MESH,
        )
        copy.start()
        return copy

    origins = [shard] + peers
    acrosses = []
    twins = []

    def take_across(index):
        acrosses[index].wait_recv()
        block = block_of(1 - column, origins[index])
        twins.append(hand_on(block, twin_send, twin_recv, shards + index, twin))

    for index, origin in enumerate(origins):
        if index:
            back_copy(index - 1, shard, origin).wait_recv()
        block = block_of(column, origin)
        acrosses.append(hand_on(block, across_send, across_recv, index, across))
        twins.append(hand_on(block, twin_send, twin_recv, index, twin))
        if index:
            take_across(index - 1)
    take_across(last)
    for copy in twins:
        copy.wait_recv()
    for copy in (
        sends
        + grad_passes
        + mom_passes
        + root_copies
        + backs
        + acrosses
        + twins
    ):
        copy.wait_send()


def by_kernel(gradient, momentum):
    block_rows, block_cols, rows, size = gradient.shape
    shards = lax.axis_size("shard")
    count = block_rows * block_cols
    flat = (count, rows, size)
    width = size // 2
    vmem = pltpu.VMEM
    dma = pltpu.SemaphoreType.DMA
    square = vmem((size, size), jnp.bfloat16)
    update, new_momentum = pl.pallas_call(
        functools.partial(step_kernel, shards, block_cols // 2),
        out_shape=[pltpu.VMEM(flat, jnp.bfloat16)] * 2,
        in_specs=[pl.BlockSpec(memory_space=pl.ANY)] * 2,
        out_specs=[pl.BlockSpec(memory_space=pltpu.VMEM)] * 2,
        scratch_shapes=[
            vmem(flat, jnp.bfloat16),
            vmem(flat, jnp.bfloat16),
            square,
            square,
            vmem((size, size), jnp.float32),
            square,
            square,
            square,
            square,
            vmem((2, size, size), jnp.bfloat16),
            vmem((size, width), jnp.float32),
            vmem((shards - 1, rows, width), jnp.bfloat16),
            dma((2,)),
            dma((2, shards)),
            dma((2, shards)),
            dma((2, shards - 1)),
            dma((2, shards - 1)),
            dma((shards - 1,)),
            dma((shards,)),
            dma((shards,)),
            dma((shards,)),
            dma((2 * shards,)),
            dma((2 * shards,)),
            dma((2,)),
            dma((2,)),
            pltpu.SemaphoreType.REGULAR((2, max(shards - 2, 1))),
        ],
        compiler_params=pltpu.CompilerParams(collective_id=0, has_side_effects=True),
    )(gradient.reshape(flat), momentum.reshape(flat))
    return (update.reshape(gradient.shape), new_momentum.reshape(gradient.shape))


def local(gradient, momentum):
    block_rows, block_cols, rows, size = gradient.shape
    shards = lax.axis_size("shard")
    fits = (
        lax.axis_size("pair") == 4
        and block_rows * block_cols == 2 * shards
        and rows * shards == size
        and shards % 2 == 0
        and rows % 32 == 0
        and size % 256 == 0
    )
    return (by_kernel if fits else by_collectives)(gradient, momentum)


def solution(mesh):
    in_specs = (P("groups", None, "shard", None), P("groups", None, "shard", None))
    out_specs = (P("groups", None, "shard", None), P("groups", None, "shard", None))
    return jax.shard_map(local, mesh=mesh, in_specs=in_specs, out_specs=out_specs, check_vma=False)
```

```python
import functools

import jax
import jax.numpy as jnp
from jax import lax
from jax.experimental import pallas as pl
from jax.experimental.pallas import tpu as pltpu
from jax.sharding import PartitionSpec as P

damping = 0.1
decay_rate = 0.9
MESH = pl.DeviceIdType.MESH


def from_partner(value, axis, apart):
    mask = 2**apart
    pairs = [(source, source ^ mask) for source in range(lax.axis_size(axis))]
    return lax.ppermute(value, axis, pairs)


def multiply(left_matrix, right_matrix):
    return jnp.dot(
        left_matrix,
        right_matrix,
        precision=lax.Precision.HIGHEST,
        preferred_element_type=jnp.float32,
    )


def gram_root(gram_matrix):
    block_size = gram_matrix.shape[0]
    identity = jnp.eye(block_size, dtype=jnp.float32)
    scaling = 2.0 * jnp.trace(gram_matrix) / block_size
    root_scale = jnp.sqrt(jnp.sqrt(scaling))
    scaled = gram_matrix / scaling
    leading = (5.0 * identity - scaled) / 4.0
    iterate = leading / root_scale
    squared = multiply(leading, leading)
    fourth = multiply(squared, squared)
    shifted = multiply(fourth, scaled)
    second = (5.0 * identity - shifted) / 4.0
    return multiply(iterate, second)


def by_collectives(gradient, momentum):
    new_momentum = (
        decay_rate * momentum.astype(jnp.float32) + gradient.astype(jnp.float32)
    ).astype(jnp.bfloat16)
    block_rows, block_cols, local_rows, block_size = gradient.shape
    half_cols = block_cols // 2
    half_width = block_size // 2
    shards = lax.axis_size("shard")
    position = lax.axis_index("pair")
    column_half = position // 2
    side_index = position % 2
    leading_side = side_index == 0
    grad_half = lax.dynamic_slice_in_dim(gradient, column_half * half_cols, half_cols, 1).reshape(
        shards, local_rows, block_size
    )
    mom_half = lax.dynamic_slice_in_dim(
        new_momentum, column_half * half_cols, half_cols, 1
    ).reshape(shards, local_rows, block_size)
    grad_recv, mom_recv = (
        lax.all_to_all(grad_half, "shard", split_axis=0, concat_axis=1, tiled=True),
        lax.all_to_all(mom_half, "shard", split_axis=0, concat_axis=1, tiled=True),
    )
    grad_block = grad_recv[0]
    mom_block = mom_recv[0]
    identity = jnp.eye(block_size, dtype=jnp.float32)
    oriented = jnp.where(leading_side, grad_block, grad_block.T)
    gram_matrix = (
        jnp.dot(oriented, oriented.T, preferred_element_type=jnp.float32) / block_size
        + damping * identity
    )
    own_root = gram_root(gram_matrix)
    partner = from_partner(own_root, "pair", 0)
    left_root = jnp.where(leading_side, own_root, partner)
    right_root = jnp.where(leading_side, partner, own_root)
    right_part = lax.dynamic_slice_in_dim(right_root, side_index * half_width, half_width, 1)
    partial_prod = multiply(mom_block.astype(jnp.float32), right_part)
    own_piece = multiply(left_root, partial_prod).astype(jnp.bfloat16)
    outgoing = own_piece.reshape(shards, local_rows, half_width)
    returned = lax.all_to_all(outgoing, "shard", split_axis=0, concat_axis=0, tiled=True)
    own_rows = returned.reshape(block_rows, half_cols, local_rows, half_width)
    gathered = lax.all_gather(own_rows[None], "pair", axis=0, tiled=True)
    update = (
        gathered.reshape(2, 2, block_rows, half_cols, local_rows, half_width)
        .transpose(2, 0, 3, 4, 1, 5)
        .reshape(block_rows, block_cols, local_rows, block_size)
    )
    return (update, new_momentum)


def dot(left, right, contract=((1,), (0,))):
    return lax.dot_general(
        left, right, (contract, ((), ())), preferred_element_type=jnp.float32
    )


def diagonal(rows, cols, offset):
    row = lax.broadcasted_iota(jnp.int32, (rows, cols), 0)
    col = lax.broadcasted_iota(jnp.int32, (rows, cols), 1)
    return row == col + offset


def step_kernel(
    shards,
    half_cols,
    grad,
    mom,
    update,
    new_mom,
    grad_rows,
    mom_rows,
    grad_block,
    mom_block,
    full,
    power1,
    power2,
    power3,
    high,
    roots,
    product,
    outgoing,
    local_sem,
    z_send,
    z_recv,
    pass_send,
    pass_recv,
    back_send,
    back_recv,
    across_send,
    across_recv,
    twin_send,
    twin_recv,
    root_send,
    root_recv,
    seen,
):
    count, rows, size = grad.shape
    half = rows // 2
    width = size // 2
    shard = lax.axis_index("shard")
    pair = lax.axis_index("pair")
    side = lax.rem(pair, 2)
    column = pair // 2
    twin = pair + 1 - 2 * side
    across = lax.rem(pair + 2, 4)
    last = shards - 1
    lower = 1 - shard // (shards // 2)
    place = lower * shard + (1 - lower) * (last - shard)
    peers = []
    for step in range(last):
        mirrored = step + (step - place + shards) // shards
        peers.append(lower * mirrored + (1 - lower) * (last - mirrored))

    def block_of(column_half, owner):
        return (owner // half_cols) * 2 * half_cols + column_half * half_cols + lax.rem(
            owner, half_cols
        )

    barrier = pltpu.get_barrier_semaphore()

    def greet(semaphore, peer):
        pl.semaphore_signal(semaphore, inc=1, device_id={"shard": peer}, device_id_type=MESH)

    @pl.when(shard > 0)
    def _():
        greet(barrier, shard - 1)

    @pl.when(shard < last)
    def _():
        greet(barrier, shard + 1)

    for peer in (twin, across):
        pl.semaphore_signal(barrier, inc=1, device_id={"pair": peer}, device_id_type=MESH)
    loads = []
    for kind, (source, local_rows) in enumerate(((grad, grad_rows), (mom, mom_rows))):
        copy = pltpu.make_async_copy(source, local_rows, local_sem.at[kind])
        copy.start()
        loads.append(copy)
    pl.semaphore_wait(barrier, 2 + (shard + last) // shards + (2 * last - shard) // shards)

    def piece(owner):
        return pl.ds(pl.multiple_of(owner * rows + side * half, half), half)

    def whole_piece(owner):
        return pl.ds(pl.multiple_of(owner * rows, rows), rows)

    own_half = pl.ds(pl.multiple_of(side * half, half), half)
    own_cols = pl.ds(pl.multiple_of(side * width, width), width)
    def row_copy(kind, target, origin):
        source, block = ((grad, grad_block), (mom, mom_block))[kind]
        return pltpu.make_async_remote_copy(
            src_ref=source.at[block_of(column, target), own_half],
            dst_ref=block.at[piece(origin)],
            send_sem=z_send.at[kind, target],
            recv_sem=z_recv.at[kind, origin],
            device_id={"shard": target},
            device_id_type=MESH,
        )

    for distance in range(1, shards):
        if distance > 1:

            @pl.when(shard >= distance - 1)
            def _():
                @pl.when(shard < last)
                def _():
                    greet(seen.at[0, distance - 2], shard + 1)

            @pl.when(shard <= last - (distance - 1))
            def _():
                @pl.when(shard > 0)
                def _():
                    greet(seen.at[1, distance - 2], shard - 1)

        @pl.when(shard <= last - distance)
        def _():
            if distance > 1:
                pl.semaphore_wait(seen.at[1, distance - 2], 1)
            row_copy(0, shard + distance, shard).start()

        @pl.when(shard >= distance)
        def _():
            if distance > 1:
                pl.semaphore_wait(seen.at[0, distance - 2], 1)
            row_copy(0, shard - distance, shard).start()

    sends = [row_copy(0, target, shard) for target in peers]
    for target in peers:
        copy = row_copy(1, target, shard)
        copy.start()
        sends.append(copy)

    def combine(momentum, gradient):
        return (
            decay_rate * momentum.astype(jnp.float32) + gradient.astype(jnp.float32)
        ).astype(jnp.bfloat16)

    for copy in loads:
        copy.wait()
    for index in range(count):
        new_mom[index] = combine(mom_rows[index], grad_rows[index])
    grad_block[whole_piece(shard), :] = grad_rows[block_of(column, shard)]

    def collect(kind, block):
        passes = []
        for index, origin in enumerate(peers):
            row_copy(kind, shard, origin).wait_recv()
            copy = pltpu.make_async_remote_copy(
                src_ref=block.at[piece(origin)],
                dst_ref=block.at[piece(origin)],
                send_sem=pass_send.at[kind, index],
                recv_sem=pass_recv.at[kind, index],
                device_id={"pair": twin},
                device_id_type=MESH,
            )
            copy.start()
            passes.append(copy)
        return passes

    grad_passes = collect(0, grad_block)
    for copy in grad_passes:
        copy.wait_recv()

    values = grad_block[...]
    wide = values.astype(jnp.float32)
    total = jnp.sum(wide * wide, keepdims=True)
    scaling = 2.0 * (total / size + damping * size) / size
    inverse = 1.0 / scaling
    identity = diagonal(size, size, 0)

    @pl.when(side == 0)
    def _():
        full[...] = dot(values, values, ((1,), (1,)))

    @pl.when(side == 1)
    def _():
        full[...] = dot(values, values, ((0,), (0,)))

    shifted = full[...] * (inverse / size) + jnp.where(identity, damping * inverse - 1.0, 0.0)
    full[...] = shifted
    power1[...] = shifted.astype(jnp.bfloat16)
    squared = dot(power1[...], power1[...])
    power2[...] = squared.astype(jnp.bfloat16)
    cubed = dot(power2[...], power1[...])
    power3[...] = cubed.astype(jnp.bfloat16)
    high[...] = (
        (35 / 1024) * full[...]
        + (-19 / 4096) * squared
        + (1 / 4096) * cubed
        - jnp.where(identity, 15 / 128, 0.0)
    ).astype(jnp.bfloat16)
    full[...] = (5 / 32) * squared - 0.25 * full[...]
    root_copies = []
    for index in range(2):
        part = pl.ds(index * width, width)
        roots[side, part, :] = (full[part, :] + dot(power3[part, :], high[...])).astype(
            jnp.bfloat16
        )
        copy = pltpu.make_async_remote_copy(
            src_ref=roots.at[side, part],
            dst_ref=roots.at[side, part],
            send_sem=root_send.at[index],
            recv_sem=root_recv.at[index],
            device_id={"pair": twin},
            device_id_type=MESH,
        )
        copy.start()
        root_copies.append(copy)

    def multiply_rows(new_rows, own_part, owner):
        product[whole_piece(owner), :] = own_part.astype(jnp.float32) + dot(
            new_rows, roots[1, :, own_cols]
        )

    own_block = block_of(column, shard)
    mom_passes = collect(1, mom_block)
    for copy in root_copies:
        copy.wait_recv()
    multiply_rows(new_mom[own_block], new_mom[own_block, :, own_cols], shard)
    for copy, origin in zip(mom_passes, peers):
        copy.wait_recv()
        new_rows = combine(mom_block[whole_piece(origin), :], grad_block[whole_piece(origin), :])
        own_part = combine(
            mom_block[whole_piece(origin), own_cols], grad_block[whole_piece(origin), own_cols]
        )
        multiply_rows(new_rows, own_part, origin)

    outer = 1.0 / jnp.sqrt(scaling)
    narrow_product = product[...].astype(jnp.bfloat16)

    def update_rows(owner):
        return (
            (
                product[whole_piece(owner), :]
                + dot(roots[0, whole_piece(owner), :], narrow_product)
            )
            * outer
        ).astype(jnp.bfloat16)

    def back_copy(index, target, origin):
        return pltpu.make_async_remote_copy(
            src_ref=outgoing.at[index],
            dst_ref=update.at[block_of(column, origin), :, own_cols],
            send_sem=back_send.at[index],
            recv_sem=back_recv.at[origin],
            device_id={"shard": target},
            device_id_type=MESH,
        )

    def hand_on(block, send, recv, index, peer):
        copy = pltpu.make_async_remote_copy(
            src_ref=update.at[block, :, own_cols],
            dst_ref=update.at[block, :, own_cols],
            send_sem=send.at[index],
            recv_sem=recv.at[index],
            device_id={"pair": peer},
            device_id_type=MESH,
        )
        copy.start()
        return copy

    acrosses = []
    twins = []

    def spread(block, index):
        acrosses.append(hand_on(block, across_send, across_recv, index, across))
        twins.append(hand_on(block, twin_send, twin_recv, index, twin))

    backs = []
    for index, target in enumerate(peers):
        outgoing[index] = update_rows(target)
        copy = back_copy(index, target, shard)
        copy.start()
        backs.append(copy)
        if index == 0:
            update[own_block, :, own_cols] = update_rows(shard)
            spread(own_block, 0)

    origins = [shard] + peers

    def take_across(index):
        acrosses[index].wait_recv()
        block = block_of(1 - column, origins[index])
        twins.append(hand_on(block, twin_send, twin_recv, shards + index, twin))

    for index in range(1, shards):
        back_copy(index - 1, shard, origins[index]).wait_recv()
        spread(block_of(column, origins[index]), index)
        take_across(index - 1)
    take_across(last)
    for copy in twins:
        copy.wait_recv()
    for copy in (
        sends
        + grad_passes
        + mom_passes
        + root_copies
        + backs
        + acrosses
        + twins
    ):
        copy.wait_send()


def by_kernel(gradient, momentum):
    block_rows, block_cols, rows, size = gradient.shape
    shards = lax.axis_size("shard")
    count = block_rows * block_cols
    flat = (count, rows, size)
    width = size // 2
    vmem = pltpu.VMEM
    dma = pltpu.SemaphoreType.DMA
    square = vmem((size, size), jnp.bfloat16)
    update, new_momentum = pl.pallas_call(
        functools.partial(step_kernel, shards, block_cols // 2),
        out_shape=[pltpu.VMEM(flat, jnp.bfloat16)] * 2,
        in_specs=[pl.BlockSpec(memory_space=pl.ANY)] * 2,
        out_specs=[pl.BlockSpec(memory_space=pltpu.VMEM)] * 2,
        scratch_shapes=[
            vmem(flat, jnp.bfloat16),
            vmem(flat, jnp.bfloat16),
            square,
            square,
            vmem((size, size), jnp.float32),
            square,
            square,
            square,
            square,
            vmem((2, size, size), jnp.bfloat16),
            vmem((size, width), jnp.float32),
            vmem((shards - 1, rows, width), jnp.bfloat16),
            dma((2,)),
            dma((2, shards)),
            dma((2, shards)),
            dma((2, shards - 1)),
            dma((2, shards - 1)),
            dma((shards - 1,)),
            dma((shards,)),
            dma((shards,)),
            dma((shards,)),
            dma((2 * shards,)),
            dma((2 * shards,)),
            dma((2,)),
            dma((2,)),
            pltpu.SemaphoreType.REGULAR((2, max(shards - 2, 1))),
        ],
        compiler_params=pltpu.CompilerParams(collective_id=0, has_side_effects=True),
    )(gradient.reshape(flat), momentum.reshape(flat))
    return (update.reshape(gradient.shape), new_momentum.reshape(gradient.shape))


def local(gradient, momentum):
    block_rows, block_cols, rows, size = gradient.shape
    shards = lax.axis_size("shard")
    fits = (
        lax.axis_size("pair") == 4
        and block_rows * block_cols == 2 * shards
        and rows * shards == size
        and shards % 2 == 0
        and rows % 32 == 0
        and size % 256 == 0
    )
    return (by_kernel if fits else by_collectives)(gradient, momentum)


def solution(mesh):
    in_specs = (P("groups", None, "shard", None), P("groups", None, "shard", None))
    out_specs = (P("groups", None, "shard", None), P("groups", None, "shard", None))
    return jax.shard_map(local, mesh=mesh, in_specs=in_specs, out_specs=out_specs, check_vma=False)
```
